32 devices in a mesh: dp: 4 (over y, core), ctx: 8 (over z, x).
Axes of the slice: x: 2, y: 2, z: 4, core: 2. Of those that a mesh axis runs over, the one named last changes fastest.
Arguments:
- inputs: float32 [4, 1024, 576], P('dp', 'ctx'), may hold values from -6 to 6
- segment_ids: int32 [4, 1024], P('dp', 'ctx'), may hold values from 0 to 2, never falling along the last dimension, each value on 1 to 512 neighbouring positions
- gain_attn: float32 [576], replicated, may hold values from 0.5 to 1.5
- gain_ffn: float32 [576], replicated, may hold values from 0.5 to 1.5
- w_query: bfloat16 [331776], P(('dp', 'ctx')), may hold values from -0.25 to 0.25
- w_key: bfloat16 [110592], P(('dp', 'ctx')), may hold values from -0.25 to 0.25
- w_value: bfloat16 [110592], P(('dp', 'ctx')), may hold values from -0.25 to 0.25
- w_out: bfloat16 [331776], P(('dp', 'ctx')), may hold values from -4 to 4
- w_gate: bfloat16 [884736], P(('dp', 'ctx')), may hold values from -0.25 to 0.25
- w_up: bfloat16 [884736], P(('dp', 'ctx')), may hold values from -0.25 to 0.25
- w_down: bfloat16 [884736], P(('dp', 'ctx')), may hold values from -0.15625 to 0.15625
- cotangent: float32 [4, 1024, 576], P('dp', 'ctx'), may hold values from -6 to 6
Outputs:
- outputs: float32 [4, 1024, 576], P('dp', 'ctx')
- grad_inputs: float32 [4, 1024, 576], P('dp', 'ctx')
- grad_gain_attn: float32 [576], replicated
- grad_gain_ffn: float32 [576], replicated
- grad_w_query: float32 [331776], P(('dp', 'ctx'))
- grad_w_key: float32 [110592], P(('dp', 'ctx'))
- grad_w_value: float32 [110592], P(('dp', 'ctx'))
- grad_w_out: float32 [331776], P(('dp', 'ctx'))
- grad_w_gate: float32 [884736], P(('dp', 'ctx'))
- grad_w_up: float32 [884736], P(('dp', 'ctx'))
- grad_w_down: float32 [884736], P(('dp', 'ctx'))
The draws below stay inside these ranges and needn't reach their ends.
Inputs may be any that keep to these rules, and one draw needn't show every extreme that they name: `segment_ids`: within a sequence the numbers never fall; a document is one run of equal numbers, of at most 512 positions.
All inputs are finite; a program needn't handle non-finite values.
Results may differ from the reference program's by a relative error of at most 0.02.
Values may be sent and summed in bfloat16 or wider, within the bound.
A program may use at most 128 MiB of HBM per device.

```python
import math
import jax
import jax.numpy as jnp
import numpy as np
from jax import lax

D = 576
H = 9
KV = 3
HD = 64
FF = 1536
SEQ = 1024
SEQS = 4


def level_of(key, dims, pieces, least, top_value):
    loudness = 1.0
    for dim, parts in pieces:
        heights = jax.random.uniform(jax.random.fold_in(jax.random.fold_in(key, 6), dim), (parts,), jnp.float32, least / len(pieces), top_value / len(pieces))
        loudness = loudness * jnp.repeat(jnp.exp(heights), dims[dim] // parts).reshape((-1,) + (1,) * (len(dims) - 1 - dim))
    return loudness


def length_profile(count, total, reach, skew):
    weights = [(1 << 20) // math.isqrt(standing ** skew) + 1 for standing in range(2, count + 1)]
    surplus, holding = total - reach - (count - 1), [1] * (count - 1)
    while surplus > 0:
        movable = [i for i in range(count - 1) if holding[i] < reach]
        mass, left = sum([weights[i] for i in movable]), surplus
        for i in movable:
            extra = min(reach - holding[i], max(1, left * weights[i] // mass), surplus)
            holding[i] = holding[i] + extra
            surplus = surplus - extra
    return np.array([reach] + holding)


def uneven(own_key, amount, total, limit, lean):
    if amount == 2:
        one = jax.random.randint(own_key, (), max(1, total - limit), min(limit, total - 1) + 1)
        return jnp.stack([one, total - one])
    lengths = jnp.asarray(length_profile(amount, total, limit, lean), jnp.int32)
    couples = (amount - 1) // 2
    donor, sink = lengths[1:1 + 2 * couples:2], lengths[2:2 + 2 * couples:2]
    slack = jnp.minimum(donor - 1, limit - sink)
    moved = jax.random.randint(jax.random.fold_in(own_key, 1), (couples,), 0, 1 << 20) % (slack + 1)
    lengths = lengths.at[1:1 + 2 * couples:2].set(donor - moved).at[2:2 + 2 * couples:2].set(sink + moved)
    return lengths[jax.random.permutation(jax.random.fold_in(own_key, 2), amount)]


def noise(own_key, extent, scale, most, pieces=(), dtype=jnp.bfloat16):
    factor_of = level_of(own_key, extent, pieces, -0.22, 0.18) if pieces else 1.0
    values = jax.random.normal(own_key, extent, jnp.float32) * scale * factor_of
    return jnp.minimum(jnp.maximum(values, -most), most).astype(dtype)


def setup_inputs(seed: int = 0) -> dict:
    seeds = jax.random.split(jax.random.key(seed), 13)
    inputs = noise(seeds[0], (SEQS, SEQ, D), 1.0, 6.0, ((0, 4), (1, 8)), jnp.float32)
    segment_ids = jax.vmap(lambda own: jnp.searchsorted(jnp.cumsum(uneven(own, max(3, SEQ // 512), SEQ, SEQ // 2, 0)), jnp.arange(SEQ), side="right"))(jax.random.split(seeds[1], SEQS)).reshape((SEQS, SEQ)).astype(jnp.int32)
    gain_attn = jnp.clip(1.0 + 0.1 * jax.random.normal(seeds[2], (D,), jnp.float32), 0.5, 1.5)
    gain_ffn = jnp.clip(1.0 + 0.1 * jax.random.normal(seeds[3], (D,), jnp.float32), 0.5, 1.5)
    w_query = noise(seeds[4], (D * H * HD,), D ** -0.5, 0.25, ((0, 32),))
    w_key = noise(seeds[5], (D * KV * HD,), D ** -0.5, 0.25, ((0, 32),))
    w_value = noise(seeds[6], (D * KV * HD,), D ** -0.5, 0.25, ((0, 32),))
    w_out = noise(seeds[7], (H * HD * D,), (max(1, H * HD // 256)) ** -0.5, 4.0, ((0, 32),))
    w_gate = noise(seeds[8], (D * FF,), D ** -0.5, 0.25, ((0, 32),))
    w_up = noise(seeds[9], (D * FF,), D ** -0.5, 0.25, ((0, 32),))
    w_down = noise(seeds[10], (FF * D,), FF ** -0.5, 0.15625, ((0, 32),))
    cotangent = noise(seeds[11], (SEQS, SEQ, D), 1.0, 6.0, ((0, 4), (1, 8)), jnp.float32)
    return dict(inputs=inputs, segment_ids=segment_ids, gain_attn=gain_attn, gain_ffn=gain_ffn, w_query=w_query, w_key=w_key, w_value=w_value, w_out=w_out, w_gate=w_gate, w_up=w_up, w_down=w_down, cotangent=cotangent)


norm_epsilon = 1e-05
rope_base = 100000.0

def matmul(left, right):
    return jnp.dot(left, right, preferred_element_type=jnp.float32)

def rope_tables(positions):
    half_size = HD // 2
    exponent = jnp.arange(half_size).astype(jnp.float32) * (2.0 / HD)
    frequency = rope_base ** (-exponent)
    angles = positions[:, None] * frequency[None, :]
    return (jnp.cos(angles), jnp.sin(angles))

def rotate(tensor, cos_table, sin_table, direction):
    half_size = HD // 2
    first_half = tensor[..., :half_size]
    second_half = tensor[..., half_size:]
    cos_wide = cos_table[:, None, :]
    sin_wide = sin_table[:, None, :] * direction
    return jnp.concatenate([first_half * cos_wide - second_half * sin_wide, second_half * cos_wide + first_half * sin_wide], axis=-1)

def norm_back(grad_norm, values_in, inverse, gain):
    scaled_in = values_in * inverse
    grad_scaled = grad_norm * gain
    grad_in = inverse * (grad_scaled - scaled_in * lax.optimization_barrier(jnp.mean(grad_scaled * scaled_in, axis=-1, keepdims=True)))
    return (grad_in, lax.optimization_barrier(jnp.sum(grad_norm * scaled_in, axis=0)))

def unpack_weights(flat):
    return (flat[0].reshape(D, H * HD), flat[1].reshape(D, KV * HD), flat[2].reshape(D, KV * HD), flat[3].reshape(H * HD, D), flat[4].reshape(D, FF), flat[5].reshape(D, FF), flat[6].reshape(FF, D))

def allowed_pairs(segments, first_row, end_row):
    same_doc = segments[first_row:end_row, None] == segments[None, :end_row]
    causal = jnp.arange(end_row)[None, :] <= jnp.arange(first_row, end_row)[:, None]
    return (same_doc & causal)[None, None]

def attend(queries, keys_all, values_all, segments):
    head_group = H // KV
    query_block = min(512, SEQ)
    scale_factor = HD ** (-0.5)
    grouped = queries.astype(jnp.float32).reshape(SEQ, KV, head_group, HD)
    key_float = keys_all.astype(jnp.float32)
    value_float = values_all.astype(jnp.float32)
    pieces_out = []
    pieces_lse = []
    for block_index in range(SEQ // query_block):
        first_row = block_index * query_block
        end_row = first_row + query_block
        scores = jnp.einsum('qkgd,skd->kgqs', grouped[first_row:end_row], key_float[:end_row]) * scale_factor
        scores = jnp.where(allowed_pairs(segments, first_row, end_row), scores, -jnp.inf)
        row_peak = lax.optimization_barrier(jnp.max(scores, axis=-1, keepdims=True))
        log_total = row_peak + jnp.log(lax.optimization_barrier(jnp.sum(jnp.exp(scores - row_peak), axis=-1, keepdims=True)))
        probs = lax.optimization_barrier(jnp.exp(scores - log_total).astype(jnp.bfloat16)).astype(jnp.float32)
        block_out = jnp.einsum('kgqs,skd->qkgd', probs, value_float[:end_row])
        pieces_out.append(block_out.reshape(query_block, H * HD))
        pieces_lse.append(log_total[..., 0])
    return (jnp.concatenate(pieces_out, axis=0).astype(jnp.bfloat16), jnp.concatenate(pieces_lse, axis=2))

def attend_back(queries, keys_all, values_all, segments, attn, log_total, grad_attn):
    head_group = H // KV
    query_block = min(512, SEQ)
    scale_factor = HD ** (-0.5)
    grouped = queries.astype(jnp.float32).reshape(SEQ, KV, head_group, HD)
    key_float = keys_all.astype(jnp.float32)
    value_float = values_all.astype(jnp.float32)
    grad_grouped = grad_attn.astype(jnp.float32).reshape(SEQ, KV, head_group, HD)
    delta = lax.optimization_barrier(jnp.sum(grad_grouped * attn.astype(jnp.float32).reshape(SEQ, KV, head_group, HD), axis=-1)).transpose(1, 2, 0)
    grad_key = jnp.zeros((SEQ, KV, HD), jnp.float32)
    grad_value = jnp.zeros((SEQ, KV, HD), jnp.float32)
    pieces_query = []
    for block_index in range(SEQ // query_block):
        first_row = block_index * query_block
        end_row = first_row + query_block
        scores = jnp.einsum('qkgd,skd->kgqs', grouped[first_row:end_row], key_float[:end_row]) * scale_factor
        scores = jnp.where(allowed_pairs(segments, first_row, end_row), scores, -jnp.inf)
        probs = jnp.exp(scores - log_total[:, :, first_row:end_row, None])
        probs_low = lax.optimization_barrier(probs.astype(jnp.bfloat16)).astype(jnp.float32)
        grad_probs = jnp.einsum('qkgd,skd->kgqs', grad_grouped[first_row:end_row], value_float[:end_row])
        grad_scores = probs * (grad_probs - delta[:, :, first_row:end_row, None])
        grad_scores = lax.optimization_barrier(grad_scores.astype(jnp.bfloat16)).astype(jnp.float32)
        pieces_query.append(jnp.einsum('kgqs,skd->qkgd', grad_scores, key_float[:end_row]) * scale_factor)
        grad_key = grad_key.at[:end_row].add(jnp.einsum('kgqs,qkgd->skd', grad_scores, grouped[first_row:end_row]) * scale_factor)
        grad_value = grad_value.at[:end_row].add(jnp.einsum('kgqs,qkgd->skd', probs_low, grad_grouped[first_row:end_row]))
    grad_query = jnp.concatenate(pieces_query, axis=0).reshape(SEQ, H, HD)
    return (grad_query, grad_key, grad_value)

def reference(inputs, segment_ids, gain_attn, gain_ffn, w_query, w_key, w_value, w_out, w_gate, w_up, w_down, cotangent):
    mat_query, mat_key, mat_value, mat_out, mat_gate, mat_up, mat_down = unpack_weights((w_query, w_key, w_value, w_out, w_gate, w_up, w_down))
    cos_table, sin_table = rope_tables(jnp.arange(SEQ).astype(jnp.float32))

    def one_sequence(carried, items):
        row_input, row_segs, row_cot = items
        inv_attn = lax.rsqrt(lax.optimization_barrier(jnp.mean(row_input * row_input, axis=-1, keepdims=True)) + norm_epsilon)
        normed_attn = (row_input * inv_attn * gain_attn).astype(jnp.bfloat16)
        queries = rotate(matmul(normed_attn, mat_query).reshape(SEQ, H, HD), cos_table, sin_table, 1.0).astype(jnp.bfloat16)
        keys_rot = rotate(matmul(normed_attn, mat_key).reshape(SEQ, KV, HD), cos_table, sin_table, 1.0).astype(jnp.bfloat16)
        values_all = matmul(normed_attn, mat_value).astype(jnp.bfloat16).reshape(SEQ, KV, HD)
        attn, log_total = attend(queries, keys_rot, values_all, row_segs)
        hidden = row_input + matmul(attn, mat_out)
        inv_ffn = lax.rsqrt(lax.optimization_barrier(jnp.mean(hidden * hidden, axis=-1, keepdims=True)) + norm_epsilon)
        normed_ffn = (hidden * inv_ffn * gain_ffn).astype(jnp.bfloat16)
        gate = matmul(normed_ffn, mat_gate)
        up_proj = matmul(normed_ffn, mat_up)
        sigma = jax.nn.sigmoid(gate)
        mixed = (gate * sigma * up_proj).astype(jnp.bfloat16)
        row_out = hidden + matmul(mixed, mat_down)
        cot_low = row_cot.astype(jnp.bfloat16)
        grad_down = matmul(mixed.T, cot_low)
        grad_mixed = matmul(cot_low, mat_down.T)
        grad_up = (grad_mixed * gate * sigma).astype(jnp.bfloat16)
        grad_gate = (grad_mixed * up_proj * sigma * (1.0 + gate * (1.0 - sigma))).astype(jnp.bfloat16)
        grad_wgate = matmul(normed_ffn.T, grad_gate)
        grad_wup = matmul(normed_ffn.T, grad_up)
        grad_normed_ffn = matmul(grad_gate, mat_gate.T) + matmul(grad_up, mat_up.T)
        grad_res_ffn, grad_gffn = norm_back(grad_normed_ffn, hidden, inv_ffn, gain_ffn)
        grad_hidden = row_cot + grad_res_ffn
        grad_hidden_low = grad_hidden.astype(jnp.bfloat16)
        grad_wout = matmul(attn.T, grad_hidden_low)
        grad_attn = matmul(grad_hidden_low, mat_out.T).astype(jnp.bfloat16)
        grad_q_rot, grad_k_rot, grad_v = attend_back(queries, keys_rot, values_all, row_segs, attn, log_total, grad_attn)
        grad_queries = rotate(grad_q_rot, cos_table, sin_table, -1.0).astype(jnp.bfloat16).reshape(SEQ, H * HD)
        grad_keys = rotate(grad_k_rot, cos_table, sin_table, -1.0).astype(jnp.bfloat16).reshape(SEQ, KV * HD)
        grad_values = grad_v.astype(jnp.bfloat16).reshape(SEQ, KV * HD)
        grad_wquery = matmul(normed_attn.T, grad_queries)
        grad_wkey = matmul(normed_attn.T, grad_keys)
        grad_wvalue = matmul(normed_attn.T, grad_values)
        grad_normed_attn = matmul(grad_queries, mat_query.T) + matmul(grad_keys, mat_key.T) + matmul(grad_values, mat_value.T)
        grad_res_attn, grad_gattn = norm_back(grad_normed_attn, row_input, inv_attn, gain_attn)
        row_grad_in = grad_hidden + grad_res_attn
        updates = (grad_wquery, grad_wkey, grad_wvalue, grad_wout, grad_wgate, grad_wup, grad_down, grad_gattn, grad_gffn)
        carried = tuple((old + new for old, new in zip(carried, updates)))
        return (carried, (row_out, row_grad_in))
    initial = (jnp.zeros((D, H * HD), jnp.float32), jnp.zeros((D, KV * HD), jnp.float32), jnp.zeros((D, KV * HD), jnp.float32), jnp.zeros((H * HD, D), jnp.float32), jnp.zeros((D, FF), jnp.float32), jnp.zeros((D, FF), jnp.float32), jnp.zeros((FF, D), jnp.float32), jnp.zeros((D,), jnp.float32), jnp.zeros((D,), jnp.float32))
    totals, stacked = lax.scan(one_sequence, initial, (inputs, segment_ids, cotangent))
    return (stacked[0], stacked[1], totals[7], totals[8], totals[0].reshape(-1), totals[1].reshape(-1), totals[2].reshape(-1), totals[3].reshape(-1), totals[4].reshape(-1), totals[5].reshape(-1), totals[6].reshape(-1))
```

```python
import jax
import jax.numpy as jnp
from jax import lax
from jax.experimental import pallas as pl
from jax.experimental.pallas import tpu as pltpu
from jax.sharding import PartitionSpec as P

D = 576
H = 9
KV = 3
HD = 64
FF = 1536


norm_epsilon = 1e-05
rope_base = 100000.0


def matmul(left, right):
    return jnp.dot(left, right, preferred_element_type=jnp.float32)


def rope_tables(positions):
    half_size = HD // 2
    exponent = jnp.arange(half_size).astype(jnp.float32) * (2.0 / HD)
    frequency = rope_base ** (-exponent)
    angles = positions[:, None] * frequency[None, :]
    return (jnp.cos(angles), jnp.sin(angles))


def rotate(tensor, cos_table, sin_table, direction):
    half_size = HD // 2
    first_half = tensor[..., :half_size]
    second_half = tensor[..., half_size:]
    cos_wide = cos_table[:, None, :]
    sin_wide = sin_table[:, None, :] * direction
    return jnp.concatenate(
        [
            first_half * cos_wide - second_half * sin_wide,
            second_half * cos_wide + first_half * sin_wide,
        ],
        axis=-1,
    )


def norm_back(grad_norm, values_in, inverse, gain):
    scaled_in = values_in * inverse
    grad_scaled = grad_norm * gain
    grad_in = inverse * (
        grad_scaled - scaled_in * jnp.mean(grad_scaled * scaled_in, axis=-1, keepdims=True)
    )
    return (grad_in, jnp.sum(grad_norm * scaled_in, axis=0))


def exchange(collective_id, *items):
    arrays = [array for array, _, _ in items]
    total = len(items)
    axes = sorted({axis for _, axis, _ in items})
    counts = {axis: lax.axis_size(axis) for axis in axes}
    most = max(counts.values())

    def kernel(*refs):
        sources, targets = refs[:total], refs[total : 2 * total]
        send_sem, recv_sem, own_sem = refs[2 * total :]
        place = {axis: lax.axis_index(axis) for axis in axes}

        def piece(index, peer):
            return sources[index] if items[index][2] else sources[index].at[peer]

        def partner(axis, step):
            return lax.rem(place[axis] + step, counts[axis])

        barrier = pltpu.get_barrier_semaphore()
        for axis in axes:
            for step in range(1, counts[axis]):
                pl.semaphore_signal(
                    barrier,
                    inc=1,
                    device_id={axis: partner(axis, step)},
                    device_id_type=pl.DeviceIdType.MESH,
                )
        started = []
        for index, (_, axis, _) in enumerate(items):
            me = place[axis]
            copy = pltpu.make_async_copy(piece(index, me), targets[index].at[me], own_sem.at[index])
            copy.start()
            started.append(copy)
        pl.semaphore_wait(barrier, sum(counts[axis] - 1 for axis in axes))
        for step in range(1, most):
            for index, (_, axis, _) in enumerate(items):
                if step >= counts[axis]:
                    continue
                peer = partner(axis, step)
                copy = pltpu.make_async_remote_copy(
                    src_ref=piece(index, peer),
                    dst_ref=targets[index].at[place[axis]],
                    send_sem=send_sem.at[index, step],
                    recv_sem=recv_sem.at[index, step],
                    device_id={axis: peer},
                    device_id_type=pl.DeviceIdType.MESH,
                )
                copy.start()
                started.append(copy)
        for copy in started:
            copy.wait()

    return pl.pallas_call(
        kernel,
        out_shape=[
            jax.ShapeDtypeStruct(
                (counts[axis],) + array.shape if whole else array.shape, array.dtype
            )
            for array, axis, whole in items
        ],
        in_specs=[pl.BlockSpec(memory_space=pl.ANY)] * total,
        out_specs=[pl.BlockSpec(memory_space=pl.ANY)] * total,
        scratch_shapes=[
            pltpu.SemaphoreType.DMA((total, most)),
            pltpu.SemaphoreType.DMA((total, most)),
            pltpu.SemaphoreType.DMA((total,)),
        ],
        compiler_params=pltpu.CompilerParams(collective_id=collective_id, has_side_effects=True),
    )(*arrays)


def pack(flat):
    lengths = [w.shape[0] for w in flat]
    if all(length % LANES == 0 for length in lengths):
        return jnp.concatenate([w.reshape(-1, LANES) for w in flat], axis=0)
    return jnp.concatenate(flat).reshape(1, -1)


def unpack(got, lengths, widths):
    out = []
    start = 0
    lanes = got.shape[-1] if got.shape[1] > 1 else 1
    rows_of = got if got.shape[1] > 1 else got.reshape(got.shape[0], -1)
    for length, width in zip(lengths, widths):
        step = length // lanes
        out.append(rows_of[:, start : start + step].reshape(-1, width))
        start += step
    return out


def pack_grads(slabs, count):
    sizes = [slab.size // count for slab in slabs]
    if all(size % LANES == 0 for size in sizes):
        return jnp.concatenate([slab.reshape(count, -1, LANES) for slab in slabs], axis=1)
    return jnp.concatenate([slab.reshape(count, 1, -1) for slab in slabs], axis=2)


def unpack_grads(own, lengths):
    out = []
    start = 0
    lanes = own.shape[-1] if own.shape[0] > 1 else 1
    rows_of = own if own.shape[0] > 1 else own.reshape(-1)
    for length in lengths:
        step = length // lanes
        out.append(rows_of[start : start + step].reshape(-1))
        start += step
    return out


def total_of(pieces):
    return jnp.sum(pieces.astype(jnp.float32), axis=0)


LANES = 128
low = jnp.bfloat16


def on_device(
    inputs,
    segment_ids,
    gain_attn,
    gain_ffn,
    w_query,
    w_key,
    w_value,
    w_out,
    w_gate,
    w_up,
    w_down,
    cotangent,
):
    head_group = H // KV
    scale_factor = HD ** (-0.5)
    span_rows = inputs.shape[1]
    dp_count = lax.axis_size("dp")
    ctx_count = lax.axis_size("ctx")
    seq_rows = span_rows * ctx_count
    key_block = min(1024, seq_rows)
    my_block = lax.axis_index("ctx")
    first_pos = my_block * span_rows
    query_pos = first_pos + jnp.arange(span_rows, dtype=jnp.int32)
    cos_table, sin_table = rope_tables(query_pos.astype(jnp.float32))
    row_input = inputs[0]
    row_segs = segment_ids[0]
    row_cot = cotangent[0]
    cot_low = row_cot.astype(low)

    attn_flat = (w_query, w_key, w_value, w_out)
    attn_lengths = [w.shape[0] for w in attn_flat]
    got_attn, got_segs, all_cot = exchange(
        1, (pack(attn_flat), "ctx", True), (segment_ids, "ctx", True), (cot_low, "dp", True)
    )
    all_cot = all_cot.reshape(-1, D)
    all_segs = got_segs.reshape(seq_rows)
    slabs = unpack(got_attn, attn_lengths, (H * HD, KV * HD, KV * HD, D))
    mat_qkv, mat_out, got_gate_up = exchange(
        2,
        (jnp.concatenate(slabs[:3], axis=1), "dp", True),
        (slabs[3], "dp", True),
        (pack((w_gate, w_up)), "ctx", True),
    )
    mat_qkv = mat_qkv.reshape(D, -1)
    mat_out = mat_out.reshape(H * HD, D)
    ff_part = FF // dp_count
    d_part = D // dp_count
    gate_up = jnp.concatenate(
        [
            slab.reshape(d_part, dp_count, ff_part)
            for slab in unpack(got_gate_up, (w_gate.shape[0], w_up.shape[0]), (FF, FF))
        ],
        axis=2,
    ).transpose(1, 0, 2)

    inv_attn = lax.rsqrt(jnp.mean(row_input * row_input, axis=-1, keepdims=True) + norm_epsilon)
    normed_attn = (row_input * inv_attn * gain_attn).astype(low)
    qkv = matmul(normed_attn, mat_qkv)
    turned = rotate(
        qkv[:, : (H + KV) * HD].reshape(span_rows, H + KV, HD), cos_table, sin_table, 1.0
    ).astype(low)
    grouped_q = turned[:, :H].reshape(span_rows, KV, head_group, HD)
    packed_kv = jnp.concatenate(
        [turned[:, H:].reshape(span_rows, KV * HD), qkv[:, (H + KV) * HD :].astype(low)], axis=1
    )
    all_kv, mat_gu = exchange(3, (packed_kv, "ctx", True), (gate_up, "dp", False))
    mat_gu = mat_gu.reshape(D, 2 * ff_part)
    all_kv = all_kv.reshape(seq_rows, 2 * KV * HD)
    all_keys = all_kv[:, : KV * HD].reshape(seq_rows, KV, HD)
    all_vals = all_kv[:, KV * HD :].reshape(seq_rows, KV, HD)

    def masked_scores(first_row, rows):
        block_keys = all_keys[first_row : first_row + rows]
        scores = (
            jnp.einsum("qkgd,skd->kgqs", grouped_q, block_keys, preferred_element_type=jnp.float32)
            * scale_factor
        )
        key_pos = first_row + jnp.arange(rows, dtype=jnp.int32)
        allowed = (row_segs[:, None] == all_segs[None, first_row : first_row + rows]) & (
            key_pos[None, :] <= query_pos[:, None]
        )
        return jnp.where(allowed[None, None], scores, -jnp.inf)

    scores = masked_scores(0, seq_rows)
    final_max = jnp.max(scores, axis=-1)
    weights_now = jnp.exp(scores - final_max[..., None])
    final_sum = jnp.sum(weights_now, axis=-1)
    final_acc = jnp.einsum(
        "kgqs,skd->kgqd", weights_now.astype(low), all_vals, preferred_element_type=jnp.float32
    )
    log_total = final_max + jnp.log(final_sum)
    attn = (
        (final_acc / final_sum[..., None])
        .transpose(2, 0, 1, 3)
        .reshape(span_rows, H * HD)
        .astype(low)
    )
    hidden = row_input + matmul(attn, mat_out)
    inv_ffn = lax.rsqrt(jnp.mean(hidden * hidden, axis=-1, keepdims=True) + norm_epsilon)
    normed_ffn = (hidden * inv_ffn * gain_ffn).astype(low)

    all_normed, got_down = exchange(
        4, (normed_ffn, "dp", True), (pack((w_down,)), "ctx", True)
    )
    (mat_down,) = unpack(got_down, (w_down.shape[0],), (D,))
    all_normed = all_normed.reshape(-1, D)
    gate_up_act = matmul(all_normed, mat_gu)
    gate = gate_up_act[:, :ff_part]
    up_proj = gate_up_act[:, ff_part:]
    sigma = jax.nn.sigmoid(gate)
    mixed = (gate * sigma * up_proj).astype(low)
    part_out = matmul(mixed, mat_down).astype(low).reshape(dp_count, span_rows, D)
    grad_mixed = matmul(all_cot, mat_down.T)
    grad_up = (grad_mixed * gate * sigma).astype(low)
    grad_gate = (grad_mixed * up_proj * sigma * (1.0 + gate * (1.0 - sigma))).astype(low)
    grad_gu_act = jnp.concatenate([grad_gate, grad_up], axis=1)
    part_normed = matmul(grad_gu_act, mat_gu.T).astype(low).reshape(dp_count, span_rows, D)
    grad_down = matmul(mixed.T, all_cot).astype(low)
    grad_gu = matmul(all_normed.T, grad_gu_act).astype(low).reshape(dp_count, d_part, -1)
    got_normed, got_down_grad = exchange(
        5, (part_normed, "dp", False), (pack_grads((grad_down,), ctx_count), "ctx", False)
    )
    grad_normed_ffn = total_of(got_normed)

    grad_res_ffn, grad_gffn = norm_back(grad_normed_ffn, hidden, inv_ffn, gain_ffn)
    grad_hidden = row_cot + grad_res_ffn
    grad_hidden_low = grad_hidden.astype(low)
    grad_out = matmul(attn.T, grad_hidden_low)
    grad_attn = matmul(grad_hidden_low, mat_out.T).astype(low)
    grad_grouped = grad_attn.reshape(span_rows, KV, head_group, HD)
    delta = jnp.sum(
        grad_grouped.astype(jnp.float32)
        * attn.reshape(span_rows, KV, head_group, HD).astype(jnp.float32),
        axis=-1,
    ).transpose(1, 2, 0)

    grad_q_rot = 0.0
    key_terms = []
    for first_row in range(0, seq_rows, key_block):
        block_keys = all_keys[first_row : first_row + key_block]
        block_vals = all_vals[first_row : first_row + key_block]
        probs = jnp.exp(masked_scores(first_row, key_block) - log_total[..., None])
        grad_probs = jnp.einsum(
            "qkgd,skd->kgqs", grad_grouped, block_vals, preferred_element_type=jnp.float32
        )
        grad_scores = (probs * (grad_probs - delta[..., None])).astype(low)
        grad_q_rot = (
            grad_q_rot
            + jnp.einsum(
                "kgqs,skd->qkgd", grad_scores, block_keys, preferred_element_type=jnp.float32
            )
            * scale_factor
        )
        grad_k_block = (
            jnp.einsum("kgqs,qkgd->skd", grad_scores, grouped_q, preferred_element_type=jnp.float32)
            * scale_factor
        )
        grad_v_block = jnp.einsum(
            "kgqs,qkgd->skd", probs.astype(low), grad_grouped, preferred_element_type=jnp.float32
        )
        key_terms.append(
            jnp.concatenate(
                [
                    grad_k_block.reshape(key_block, KV * HD),
                    grad_v_block.reshape(key_block, KV * HD),
                ],
                axis=1,
            ).astype(low)
        )
    key_terms = jnp.concatenate(key_terms, axis=0).reshape(ctx_count, span_rows, 2 * KV * HD)
    got_terms, got_out, got_gu, got_out_grad = exchange(
        6,
        (key_terms, "ctx", False),
        (part_out, "dp", False),
        (grad_gu, "dp", False),
        (grad_out.astype(low).reshape(dp_count, H * HD // dp_count, D), "dp", False),
    )
    out_rows = hidden + total_of(got_out)
    slab_gate = got_gu[:, :, :ff_part].transpose(1, 0, 2).reshape(d_part, FF)
    slab_up = got_gu[:, :, ff_part:].transpose(1, 0, 2).reshape(d_part, FF)
    slab_out = total_of(got_out_grad).astype(low)
    own_grads = total_of(got_terms)
    grad_qk = rotate(
        jnp.concatenate(
            [
                grad_q_rot.reshape(span_rows, H, HD),
                own_grads[:, : KV * HD].reshape(span_rows, KV, HD),
            ],
            axis=1,
        ),
        cos_table,
        sin_table,
        -1.0,
    )
    grad_qkv = jnp.concatenate(
        [grad_qk.reshape(span_rows, (H + KV) * HD).astype(low), own_grads[:, KV * HD :].astype(low)],
        axis=1,
    )
    grad_mat_qkv = matmul(normed_attn.T, grad_qkv)
    grad_normed_attn = matmul(grad_qkv, mat_qkv.T)
    grad_res_attn, grad_gattn = norm_back(grad_normed_attn, row_input, inv_attn, gain_attn)
    grad_rows = grad_hidden + grad_res_attn

    gain_terms = jnp.stack([grad_gattn, grad_gffn])
    got_gains, got_qkv, got_gu_grad = exchange(
        7,
        (gain_terms, "dp", True),
        (grad_mat_qkv.astype(low).reshape(dp_count, d_part, -1), "dp", False),
        (pack_grads((slab_gate, slab_up), ctx_count), "ctx", False),
    )
    slab_qkv = total_of(got_qkv).astype(low)
    attn_slabs = (
        slab_qkv[:, : H * HD],
        slab_qkv[:, H * HD : (H + KV) * HD],
        slab_qkv[:, (H + KV) * HD :],
        slab_out,
    )
    got_gains, got_attn_grad = exchange(
        8,
        (total_of(got_gains), "ctx", True),
        (pack_grads(attn_slabs, ctx_count), "ctx", False),
    )
    gains = total_of(got_gains)
    reduced = (
        unpack_grads(total_of(got_attn_grad), attn_lengths)
        + unpack_grads(total_of(got_gu_grad), (w_gate.shape[0], w_up.shape[0]))
        + unpack_grads(total_of(got_down_grad), (w_down.shape[0],))
    )
    return (out_rows[None], grad_rows[None], gains[0], gains[1], *reduced)


def solution(mesh):
    return jax.shard_map(
        on_device,
        mesh=mesh,
        in_specs=(
            P("dp", "ctx", None),
            P("dp", "ctx"),
            P(),
            P(),
            P(("dp", "ctx")),
            P(("dp", "ctx")),
            P(("dp", "ctx")),
            P(("dp", "ctx")),
            P(("dp", "ctx")),
            P(("dp", "ctx")),
            P(("dp", "ctx")),
            P("dp", "ctx", None),
        ),
        out_specs=(
            P("dp", "ctx", None),
            P("dp", "ctx", None),
            P(),
            P(),
            P(("dp", "ctx")),
            P(("dp", "ctx")),
            P(("dp", "ctx")),
            P(("dp", "ctx")),
            P(("dp", "ctx")),
            P(("dp", "ctx")),
            P(("dp", "ctx")),
        ),
        check_vma=False,
    )
```

```python
import jax
import jax.numpy as jnp
from jax import lax
from jax.experimental import pallas as pl
from jax.experimental.pallas import tpu as pltpu
from jax.sharding import PartitionSpec as P

D = 576
H = 9
KV = 3
HD = 64
FF = 1536


norm_epsilon = 1e-05
rope_base = 100000.0


def matmul(left, right):
    return jnp.dot(left, right, preferred_element_type=jnp.float32)


def rope_tables(positions):
    half_size = HD // 2
    exponent = jnp.arange(half_size).astype(jnp.float32) * (2.0 / HD)
    frequency = rope_base ** (-exponent)
    angles = positions[:, None] * frequency[None, :]
    return (jnp.cos(angles), jnp.sin(angles))


def rotate(tensor, cos_table, sin_table, direction):
    half_size = HD // 2
    first_half = tensor[..., :half_size]
    second_half = tensor[..., half_size:]
    cos_wide = cos_table[:, None, :]
    sin_wide = sin_table[:, None, :] * direction
    return jnp.concatenate(
        [
            first_half * cos_wide - second_half * sin_wide,
            second_half * cos_wide + first_half * sin_wide,
        ],
        axis=-1,
    )


def norm_back(grad_norm, values_in, inverse, gain):
    scaled_in = values_in * inverse
    grad_scaled = grad_norm * gain
    grad_in = inverse * (
        grad_scaled - scaled_in * jnp.mean(grad_scaled * scaled_in, axis=-1, keepdims=True)
    )
    return (grad_in, jnp.sum(grad_norm * scaled_in, axis=0))


def exchange(collective_id, *items):
    arrays = []
    counts = {axis: lax.axis_size(axis) for _, axis, _ in items}
    axes = sorted(counts)
    shapes = []
    staging = []
    slot_of = {}
    for index, (array, axis, mode) in enumerate(items):
        count = counts[axis]
        shape = array.shape
        if mode == "gather":
            shape = (count,) + shape
        elif mode == "sum":
            array = array.reshape((count // 2, 2) + shape[1:])
            shape = (count // 2,) + shape[1:]
            slot_of[index] = len(staging)
            staging += [pltpu.VMEM(shape, array.dtype), pltpu.VMEM(shape, array.dtype)]
        arrays.append(array)
        shapes.append(jax.ShapeDtypeStruct(shape, array.dtype))
    total = len(items)
    most = max(counts.values())

    def kernel(*refs):
        sources, targets = refs[:total], refs[total : 2 * total]
        send_sem, recv_sem, own_sem = refs[2 * total : 2 * total + 3]
        stages = refs[2 * total + 3 :]
        place = {axis: lax.axis_index(axis) for axis in axes}

        def ahead(axis, step):
            return lax.rem(place[axis] + step + counts[axis], counts[axis])

        def sibling(axis):
            return place[axis] + 1 - 2 * lax.rem(place[axis], 2)

        def remote(source, target, index, slot, peer):
            copy = pltpu.make_async_remote_copy(
                src_ref=source,
                dst_ref=target,
                send_sem=send_sem.at[index, slot],
                recv_sem=recv_sem.at[index, slot],
                device_id={items[index][1]: peer},
                device_id_type=pl.DeviceIdType.MESH,
            )
            copy.start()
            return copy

        barrier = pltpu.get_barrier_semaphore()
        greeted = 0
        for axis in axes:
            whole = any(mode == "swap" and axis == other for _, other, mode in items)
            steps = range(1, counts[axis]) if whole else range(2, counts[axis], 2)
            peers = [ahead(axis, step) for step in steps]
            if not whole:
                peers.append(sibling(axis))
            for peer in peers:
                pl.semaphore_signal(
                    barrier, inc=1, device_id={axis: peer}, device_id_type=pl.DeviceIdType.MESH
                )
            greeted += len(peers)
        open_copies = []
        loads = {}
        for index, (_, axis, mode) in enumerate(items):
            me = place[axis]
            if mode == "sum":
                copy = pltpu.make_async_copy(
                    sources[index].at[:, lax.rem(me, 2)],
                    stages[slot_of[index]],
                    own_sem.at[index, 0],
                )
                loads[index] = [copy]
            else:
                own = sources[index] if mode == "gather" else sources[index].at[me]
                copy = pltpu.make_async_copy(own, targets[index].at[me], own_sem.at[index, 0])
                open_copies.append(copy)
            copy.start()
        pl.semaphore_wait(barrier, greeted)
        arriving = {}
        for index, (_, axis, mode) in enumerate(items):
            me = place[axis]
            if mode == "sum":
                loads[index].append(
                    remote(
                        sources[index].at[:, 1 - lax.rem(me, 2)],
                        stages[slot_of[index] + 1],
                        index,
                        0,
                        sibling(axis),
                    )
                )
            elif mode == "gather":
                for step in range(2, counts[axis], 2):
                    arriving[index, step] = remote(
                        sources[index], targets[index].at[me], index, step, ahead(axis, step)
                    )
                open_copies.append(
                    remote(sources[index], targets[index].at[me], index, 1, sibling(axis))
                )
        for index, (_, axis, mode) in enumerate(items):
            if mode == "swap":
                for step in range(1, counts[axis]):
                    peer = ahead(axis, step)
                    open_copies.append(
                        remote(
                            sources[index].at[peer],
                            targets[index].at[place[axis]],
                            index,
                            step,
                            peer,
                        )
                    )
        for index, (_, axis, mode) in enumerate(items):
            if mode != "sum":
                continue
            mine, other = stages[slot_of[index]], stages[slot_of[index] + 1]
            for copy in loads[index]:
                copy.wait()

            def add(row, carry):
                mine[row] = (
                    mine[row].astype(jnp.float32) + other[row].astype(jnp.float32)
                ).astype(mine.dtype)
                return carry

            lax.fori_loop(0, counts[axis] // 2, add, 0)
            here = place[axis] // 2
            for step in range(2, counts[axis], 2):
                peer = ahead(axis, step)
                open_copies.append(
                    remote(mine.at[peer // 2], targets[index].at[here], index, step, peer)
                )
            copy = pltpu.make_async_copy(
                mine.at[here], targets[index].at[here], own_sem.at[index, 1]
            )
            copy.start()
            open_copies.append(copy)
        for step in range(2, most, 2):
            for index, (_, axis, mode) in enumerate(items):
                if mode == "gather" and step < counts[axis]:
                    arriving[index, step].wait_recv()
                    block = targets[index].at[ahead(axis, -step)]
                    open_copies.append(remote(block, block, index, step + 1, sibling(axis)))
        for copy in arriving.values():
            copy.wait_send()
        for copy in open_copies:
            copy.wait()

    return pl.pallas_call(
        kernel,
        out_shape=shapes,
        in_specs=[pl.BlockSpec(memory_space=pl.ANY)] * total,
        out_specs=[pl.BlockSpec(memory_space=pl.ANY)] * total,
        scratch_shapes=[
            pltpu.SemaphoreType.DMA((total, most)),
            pltpu.SemaphoreType.DMA((total, most)),
            pltpu.SemaphoreType.DMA((total, 2)),
        ]
        + staging,
        compiler_params=pltpu.CompilerParams(collective_id=collective_id, has_side_effects=True),
    )(*arrays)


def pack(flat):
    lengths = [w.shape[0] for w in flat]
    if all(length % LANES == 0 for length in lengths):
        return jnp.concatenate([w.reshape(-1, LANES) for w in flat], axis=0)
    return jnp.concatenate(flat).reshape(1, -1)


def unpack(got, lengths, widths):
    out = []
    start = 0
    lanes = got.shape[-1] if got.shape[1] > 1 else 1
    rows_of = got if got.shape[1] > 1 else got.reshape(got.shape[0], -1)
    for length, width in zip(lengths, widths):
        step = length // lanes
        out.append(rows_of[:, start : start + step].reshape(-1, width))
        start += step
    return out


def pack_grads(slabs, count):
    sizes = [slab.size // count for slab in slabs]
    if all(size % LANES == 0 for size in sizes):
        return jnp.concatenate([slab.reshape(count, -1, LANES) for slab in slabs], axis=1)
    return jnp.concatenate([slab.reshape(count, 1, -1) for slab in slabs], axis=2)


def unpack_grads(own, lengths):
    out = []
    start = 0
    lanes = own.shape[-1] if own.shape[0] > 1 else 1
    rows_of = own if own.shape[0] > 1 else own.reshape(-1)
    for length in lengths:
        step = length // lanes
        out.append(rows_of[start : start + step].reshape(-1))
        start += step
    return out


def total_of(pieces):
    return jnp.sum(pieces.astype(jnp.float32), axis=0)


LANES = 128
low = jnp.bfloat16


def on_device(
    inputs,
    segment_ids,
    gain_attn,
    gain_ffn,
    w_query,
    w_key,
    w_value,
    w_out,
    w_gate,
    w_up,
    w_down,
    cotangent,
):
    head_group = H // KV
    scale_factor = HD ** (-0.5)
    span_rows = inputs.shape[1]
    dp_count = lax.axis_size("dp")
    ctx_count = lax.axis_size("ctx")
    seq_rows = span_rows * ctx_count
    key_block = min(1024, seq_rows)
    my_block = lax.axis_index("ctx")
    first_pos = my_block * span_rows
    query_pos = first_pos + jnp.arange(span_rows, dtype=jnp.int32)
    cos_table, sin_table = rope_tables(query_pos.astype(jnp.float32))
    row_input = inputs[0]
    row_segs = segment_ids[0]
    row_cot = cotangent[0]
    cot_low = row_cot.astype(low)

    attn_flat = (w_query, w_key, w_value, w_out)
    attn_lengths = [w.shape[0] for w in attn_flat]
    got_attn, got_segs, all_cot = exchange(
        1, (pack(attn_flat), "ctx", "gather"), (segment_ids, "ctx", "gather"), (cot_low, "dp", "gather")
    )
    all_cot = all_cot.reshape(-1, D)
    all_segs = got_segs.reshape(seq_rows)
    slabs = unpack(got_attn, attn_lengths, (H * HD, KV * HD, KV * HD, D))
    mat_qkv, mat_out, got_gate_up = exchange(
        2,
        (jnp.concatenate(slabs[:3], axis=1), "dp", "gather"),
        (slabs[3], "dp", "gather"),
        (pack((w_gate, w_up)), "ctx", "gather"),
    )
    mat_qkv = mat_qkv.reshape(D, -1)
    mat_out = mat_out.reshape(H * HD, D)
    ff_part = FF // dp_count
    d_part = D // dp_count
    gate_up = jnp.concatenate(
        [
            slab.reshape(d_part, dp_count, ff_part)
            for slab in unpack(got_gate_up, (w_gate.shape[0], w_up.shape[0]), (FF, FF))
        ],
        axis=2,
    ).transpose(1, 0, 2)

    inv_attn = lax.rsqrt(jnp.mean(row_input * row_input, axis=-1, keepdims=True) + norm_epsilon)
    normed_attn = (row_input * inv_attn * gain_attn).astype(low)
    qkv = matmul(normed_attn, mat_qkv)
    turned = rotate(
        qkv[:, : (H + KV) * HD].reshape(span_rows, H + KV, HD), cos_table, sin_table, 1.0
    ).astype(low)
    grouped_q = turned[:, :H].reshape(span_rows, KV, head_group, HD)
    packed_kv = jnp.concatenate(
        [turned[:, H:].reshape(span_rows, KV * HD), qkv[:, (H + KV) * HD :].astype(low)], axis=1
    )
    all_kv, mat_gu = exchange(3, (packed_kv, "ctx", "gather"), (gate_up, "dp", "swap"))
    mat_gu = mat_gu.reshape(D, 2 * ff_part)
    all_kv = all_kv.reshape(seq_rows, 2 * KV * HD)
    all_keys = all_kv[:, : KV * HD].reshape(seq_rows, KV, HD)
    all_vals = all_kv[:, KV * HD :].reshape(seq_rows, KV, HD)

    def masked_scores(first_row, rows):
        block_keys = all_keys[first_row : first_row + rows]
        scores = (
            jnp.einsum("qkgd,skd->kgqs", grouped_q, block_keys, preferred_element_type=jnp.float32)
            * scale_factor
        )
        key_pos = first_row + jnp.arange(rows, dtype=jnp.int32)
        allowed = (row_segs[:, None] == all_segs[None, first_row : first_row + rows]) & (
            key_pos[None, :] <= query_pos[:, None]
        )
        return jnp.where(allowed[None, None], scores, -jnp.inf)

    scores = masked_scores(0, seq_rows)
    final_max = jnp.max(scores, axis=-1)
    weights_now = jnp.exp(scores - final_max[..., None])
    final_sum = jnp.sum(weights_now, axis=-1)
    final_acc = jnp.einsum(
        "kgqs,skd->kgqd", weights_now.astype(low), all_vals, preferred_element_type=jnp.float32
    )
    log_total = final_max + jnp.log(final_sum)
    attn = (
        (final_acc / final_sum[..., None])
        .transpose(2, 0, 1, 3)
        .reshape(span_rows, H * HD)
        .astype(low)
    )
    hidden = row_input + matmul(attn, mat_out)
    inv_ffn = lax.rsqrt(jnp.mean(hidden * hidden, axis=-1, keepdims=True) + norm_epsilon)
    normed_ffn = (hidden * inv_ffn * gain_ffn).astype(low)

    all_normed, got_down = exchange(
        4, (normed_ffn, "dp", "gather"), (pack((w_down,)), "ctx", "gather")
    )
    (mat_down,) = unpack(got_down, (w_down.shape[0],), (D,))
    all_normed = all_normed.reshape(-1, D)
    gate_up_act = matmul(all_normed, mat_gu)
    gate = gate_up_act[:, :ff_part]
    up_proj = gate_up_act[:, ff_part:]
    sigma = jax.nn.sigmoid(gate)
    mixed = (gate * sigma * up_proj).astype(low)
    part_out = matmul(mixed, mat_down).astype(low).reshape(dp_count, span_rows, D)
    grad_mixed = matmul(all_cot, mat_down.T)
    grad_up = (grad_mixed * gate * sigma).astype(low)
    grad_gate = (grad_mixed * up_proj * sigma * (1.0 + gate * (1.0 - sigma))).astype(low)
    grad_gu_act = jnp.concatenate([grad_gate, grad_up], axis=1)
    part_normed = matmul(grad_gu_act, mat_gu.T).astype(low).reshape(dp_count, span_rows, D)
    grad_down = matmul(mixed.T, all_cot).astype(low)
    grad_gu = matmul(all_normed.T, grad_gu_act).astype(low).reshape(dp_count, d_part, -1)
    got_normed, got_down_grad = exchange(
        5, (part_normed, "dp", "sum"), (pack_grads((grad_down,), ctx_count), "ctx", "sum")
    )
    grad_normed_ffn = total_of(got_normed)

    grad_res_ffn, grad_gffn = norm_back(grad_normed_ffn, hidden, inv_ffn, gain_ffn)
    grad_hidden = row_cot + grad_res_ffn
    grad_hidden_low = grad_hidden.astype(low)
    grad_out = matmul(attn.T, grad_hidden_low)
    grad_attn = matmul(grad_hidden_low, mat_out.T).astype(low)
    grad_grouped = grad_attn.reshape(span_rows, KV, head_group, HD)
    delta = jnp.sum(
        grad_grouped.astype(jnp.float32)
        * attn.reshape(span_rows, KV, head_group, HD).astype(jnp.float32),
        axis=-1,
    ).transpose(1, 2, 0)

    grad_q_rot = 0.0
    key_terms = []
    for first_row in range(0, seq_rows, key_block):
        block_keys = all_keys[first_row : first_row + key_block]
        block_vals = all_vals[first_row : first_row + key_block]
        probs = jnp.exp(masked_scores(first_row, key_block) - log_total[..., None])
        grad_probs = jnp.einsum(
            "qkgd,skd->kgqs", grad_grouped, block_vals, preferred_element_type=jnp.float32
        )
        grad_scores = (probs * (grad_probs - delta[..., None])).astype(low)
        grad_q_rot = (
            grad_q_rot
            + jnp.einsum(
                "kgqs,skd->qkgd", grad_scores, block_keys, preferred_element_type=jnp.float32
            )
            * scale_factor
        )
        grad_k_block = (
            jnp.einsum("kgqs,qkgd->skd", grad_scores, grouped_q, preferred_element_type=jnp.float32)
            * scale_factor
        )
        grad_v_block = jnp.einsum(
            "kgqs,qkgd->skd", probs.astype(low), grad_grouped, preferred_element_type=jnp.float32
        )
        key_terms.append(
            jnp.concatenate(
                [
                    grad_k_block.reshape(key_block, KV * HD),
                    grad_v_block.reshape(key_block, KV * HD),
                ],
                axis=1,
            ).astype(low)
        )
    key_terms = jnp.concatenate(key_terms, axis=0).reshape(ctx_count, span_rows, 2 * KV * HD)
    got_terms, got_gu = exchange(6, (key_terms, "ctx", "sum"), (grad_gu, "dp", "swap"))
    slab_gate = got_gu[:, :, :ff_part].transpose(1, 0, 2).reshape(d_part, FF)
    slab_up = got_gu[:, :, ff_part:].transpose(1, 0, 2).reshape(d_part, FF)
    own_grads = total_of(got_terms)
    grad_qk = rotate(
        jnp.concatenate(
            [
                grad_q_rot.reshape(span_rows, H, HD),
                own_grads[:, : KV * HD].reshape(span_rows, KV, HD),
            ],
            axis=1,
        ),
        cos_table,
        sin_table,
        -1.0,
    )
    grad_qkv = jnp.concatenate(
        [grad_qk.reshape(span_rows, (H + KV) * HD).astype(low), own_grads[:, KV * HD :].astype(low)],
        axis=1,
    )
    grad_mat_qkv = matmul(normed_attn.T, grad_qkv)
    grad_normed_attn = matmul(grad_qkv, mat_qkv.T)
    grad_res_attn, grad_gattn = norm_back(grad_normed_attn, row_input, inv_attn, gain_attn)
    grad_rows = grad_hidden + grad_res_attn

    gain_terms = jnp.stack([grad_gattn, grad_gffn])
    got_gains, got_qkv, got_out_grad, got_gu_grad = exchange(
        7,
        (gain_terms, "dp", "gather"),
        (grad_mat_qkv.astype(low).reshape(dp_count, d_part, -1), "dp", "sum"),
        (grad_out.astype(low).reshape(dp_count, H * HD // dp_count, D), "dp", "sum"),
        (pack_grads((slab_gate, slab_up), ctx_count), "ctx", "sum"),
    )
    slab_qkv = total_of(got_qkv).astype(low)
    slab_out = total_of(got_out_grad).astype(low)
    attn_slabs = (
        slab_qkv[:, : H * HD],
        slab_qkv[:, H * HD : (H + KV) * HD],
        slab_qkv[:, (H + KV) * HD :],
        slab_out,
    )
    got_gains, got_out, got_attn_grad = exchange(
        8,
        (total_of(got_gains), "ctx", "gather"),
        (part_out, "dp", "sum"),
        (pack_grads(attn_slabs, ctx_count), "ctx", "sum"),
    )
    gains = total_of(got_gains)
    out_rows = hidden + total_of(got_out)
    reduced = (
        unpack_grads(total_of(got_attn_grad), attn_lengths)
        + unpack_grads(total_of(got_gu_grad), (w_gate.shape[0], w_up.shape[0]))
        + unpack_grads(total_of(got_down_grad), (w_down.shape[0],))
    )
    return (out_rows[None], grad_rows[None], gains[0], gains[1], *reduced)


def solution(mesh):
    return jax.shard_map(
        on_device,
        mesh=mesh,
        in_specs=(
            P("dp", "ctx", None),
            P("dp", "ctx"),
            P(),
            P(),
            P(("dp", "ctx")),
            P(("dp", "ctx")),
            P(("dp", "ctx")),
            P(("dp", "ctx")),
            P(("dp", "ctx")),
            P(("dp", "ctx")),
            P(("dp", "ctx")),
            P("dp", "ctx", None),
        ),
        out_specs=(
            P("dp", "ctx", None),
            P("dp", "ctx", None),
            P(),
            P(),
            P(("dp", "ctx")),
            P(("dp", "ctx")),
            P(("dp", "ctx")),
            P(("dp", "ctx")),
            P(("dp", "ctx")),
            P(("dp", "ctx")),
            P(("dp", "ctx")),
        ),
        check_vma=False,
    )
```

```python
import jax
import jax.numpy as jnp
from jax import lax
from jax.experimental import pallas as pl
from jax.experimental.pallas import tpu as pltpu
from jax.sharding import PartitionSpec as P

D = 576
H = 9
KV = 3
HD = 64
FF = 1536


norm_epsilon = 1e-05
rope_base = 100000.0


def matmul(left, right):
    return jnp.dot(left, right, preferred_element_type=jnp.float32)


def rope_tables(positions):
    half_size = HD // 2
    exponent = jnp.arange(half_size).astype(jnp.float32) * (2.0 / HD)
    frequency = rope_base ** (-exponent)
    angles = positions[:, None] * frequency[None, :]
    return (jnp.cos(angles), jnp.sin(angles))


def rotate(tensor, cos_table, sin_table, direction):
    half_size = HD // 2
    first_half = tensor[..., :half_size]
    second_half = tensor[..., half_size:]
    cos_wide = cos_table[:, None, :]
    sin_wide = sin_table[:, None, :] * direction
    return jnp.concatenate(
        [
            first_half * cos_wide - second_half * sin_wide,
            second_half * cos_wide + first_half * sin_wide,
        ],
        axis=-1,
    )


def norm_back(grad_norm, values_in, inverse, gain):
    scaled_in = values_in * inverse
    grad_scaled = grad_norm * gain
    grad_in = inverse * (
        grad_scaled - scaled_in * jnp.mean(grad_scaled * scaled_in, axis=-1, keepdims=True)
    )
    return (grad_in, jnp.sum(grad_norm * scaled_in, axis=0))


def exchange(collective_id, *items):
    arrays = []
    counts = {axis: lax.axis_size(axis) for _, axis, _ in items}
    axes = sorted(counts)
    shapes = []
    staging = []
    slot_of = {}
    for index, (array, axis, mode) in enumerate(items):
        count = counts[axis]
        shape = array.shape
        if mode == "gather":
            shape = (count,) + shape
        elif mode == "sum":
            array = array.reshape((count // 2, 2) + shape[1:])
            shape = (count // 2,) + shape[1:]
            slot_of[index] = len(staging)
            staging += [pltpu.VMEM(shape, array.dtype), pltpu.VMEM(shape, array.dtype)]
        arrays.append(array)
        shapes.append(jax.ShapeDtypeStruct(shape, array.dtype))
    total = len(items)
    most = max(counts.values())

    def kernel(*refs):
        sources, targets = refs[:total], refs[total : 2 * total]
        send_sem, recv_sem, own_sem = refs[2 * total : 2 * total + 3]
        stages = refs[2 * total + 3 :]
        place = {axis: lax.axis_index(axis) for axis in axes}

        def ahead(axis, step):
            return lax.rem(place[axis] + step + counts[axis], counts[axis])

        def sibling(axis):
            return place[axis] + 1 - 2 * lax.rem(place[axis], 2)

        def remote(source, target, index, slot, peer):
            copy = pltpu.make_async_remote_copy(
                src_ref=source,
                dst_ref=target,
                send_sem=send_sem.at[index, slot],
                recv_sem=recv_sem.at[index, slot],
                device_id={items[index][1]: peer},
                device_id_type=pl.DeviceIdType.MESH,
            )
            copy.start()
            return copy

        barrier = pltpu.get_barrier_semaphore()
        greeted = 0
        for axis in axes:
            whole = any(mode == "swap" and axis == other for _, other, mode in items)
            steps = range(1, counts[axis]) if whole else range(2, counts[axis], 2)
            peers = [ahead(axis, step) for step in steps]
            if not whole:
                peers.append(sibling(axis))
            for peer in peers:
                pl.semaphore_signal(
                    barrier, inc=1, device_id={axis: peer}, device_id_type=pl.DeviceIdType.MESH
                )
            greeted += len(peers)
        open_copies = []
        loads = {}
        for index, (_, axis, mode) in enumerate(items):
            me = place[axis]
            if mode == "sum":
                copy = pltpu.make_async_copy(
                    sources[index].at[:, lax.rem(me, 2)],
                    stages[slot_of[index]],
                    own_sem.at[index, 0],
                )
                loads[index] = [copy]
            else:
                own = sources[index] if mode == "gather" else sources[index].at[me]
                copy = pltpu.make_async_copy(own, targets[index].at[me], own_sem.at[index, 0])
                open_copies.append(copy)
            copy.start()
        pl.semaphore_wait(barrier, greeted)
        arriving = {}
        for index, (_, axis, mode) in enumerate(items):
            me = place[axis]
            if mode == "sum":
                loads[index].append(
                    remote(
                        sources[index].at[:, 1 - lax.rem(me, 2)],
                        stages[slot_of[index] + 1],
                        index,
                        0,
                        sibling(axis),
                    )
                )
            elif mode == "gather":
                for step in range(2, counts[axis], 2):
                    arriving[index, step] = remote(
                        sources[index], targets[index].at[me], index, step, ahead(axis, step)
                    )
                open_copies.append(
                    remote(sources[index], targets[index].at[me], index, 1, sibling(axis))
                )
        for index, (_, axis, mode) in enumerate(items):
            if mode == "swap":
                for step in range(1, counts[axis]):
                    peer = ahead(axis, step)
                    open_copies.append(
                        remote(
                            sources[index].at[peer],
                            targets[index].at[place[axis]],
                            index,
                            step,
                            peer,
                        )
                    )
        for index, (_, axis, mode) in enumerate(items):
            if mode != "sum":
                continue
            mine, other = stages[slot_of[index]], stages[slot_of[index] + 1]
            for copy in loads[index]:
                copy.wait()

            def add(row, carry):
                mine[row] = (
                    mine[row].astype(jnp.float32) + other[row].astype(jnp.float32)
                ).astype(mine.dtype)
                return carry

            lax.fori_loop(0, counts[axis] // 2, add, 0)
            here = place[axis] // 2
            for step in range(2, counts[axis], 2):
                peer = ahead(axis, step)
                open_copies.append(
                    remote(mine.at[peer // 2], targets[index].at[here], index, step, peer)
                )
            copy = pltpu.make_async_copy(
                mine.at[here], targets[index].at[here], own_sem.at[index, 1]
            )
            copy.start()
            open_copies.append(copy)
        for step in range(2, most, 2):
            for index, (_, axis, mode) in enumerate(items):
                if mode == "gather" and step < counts[axis]:
                    arriving[index, step].wait_recv()
                    block = targets[index].at[ahead(axis, -step)]
                    open_copies.append(remote(block, block, index, step + 1, sibling(axis)))
        for copy in arriving.values():
            copy.wait_send()
        for copy in open_copies:
            copy.wait()

    return pl.pallas_call(
        kernel,
        out_shape=shapes,
        in_specs=[pl.BlockSpec(memory_space=pl.ANY)] * total,
        out_specs=[pl.BlockSpec(memory_space=pl.ANY)] * total,
        scratch_shapes=[
            pltpu.SemaphoreType.DMA((total, most)),
            pltpu.SemaphoreType.DMA((total, most)),
            pltpu.SemaphoreType.DMA((total, 2)),
        ]
        + staging,
        compiler_params=pltpu.CompilerParams(collective_id=collective_id, has_side_effects=True),
    )(*arrays)


def pack(flat):
    lengths = [w.shape[0] for w in flat]
    if all(length % LANES == 0 for length in lengths):
        return jnp.concatenate([w.reshape(-1, LANES) for w in flat], axis=0)
    return jnp.concatenate(flat).reshape(1, -1)


def unpack(got, lengths, widths):
    out = []
    start = 0
    lanes = got.shape[-1] if got.shape[1] > 1 else 1
    rows_of = got if got.shape[1] > 1 else got.reshape(got.shape[0], -1)
    for length, width in zip(lengths, widths):
        step = length // lanes
        out.append(rows_of[:, start : start + step].reshape(-1, width))
        start += step
    return out


def pack_grads(slabs, count):
    sizes = [slab.size // count for slab in slabs]
    if all(size % LANES == 0 for size in sizes):
        return jnp.concatenate([slab.reshape(count, -1, LANES) for slab in slabs], axis=1)
    return jnp.concatenate([slab.reshape(count, 1, -1) for slab in slabs], axis=2)


def unpack_grads(own, lengths):
    out = []
    start = 0
    lanes = own.shape[-1] if own.shape[0] > 1 else 1
    rows_of = own if own.shape[0] > 1 else own.reshape(-1)
    for length in lengths:
        step = length // lanes
        out.append(rows_of[start : start + step].reshape(-1))
        start += step
    return out


def total_of(pieces):
    return jnp.sum(pieces.astype(jnp.float32), axis=0)


LANES = 128
low = jnp.bfloat16


def on_device(
    inputs,
    segment_ids,
    gain_attn,
    gain_ffn,
    w_query,
    w_key,
    w_value,
    w_out,
    w_gate,
    w_up,
    w_down,
    cotangent,
):
    head_group = H // KV
    scale_factor = HD ** (-0.5)
    span_rows = inputs.shape[1]
    dp_count = lax.axis_size("dp")
    ctx_count = lax.axis_size("ctx")
    seq_rows = span_rows * ctx_count
    key_block = min(1024, seq_rows)
    my_block = lax.axis_index("ctx")
    first_pos = my_block * span_rows
    query_pos = first_pos + jnp.arange(span_rows, dtype=jnp.int32)
    cos_table, sin_table = rope_tables(query_pos.astype(jnp.float32))
    row_input = inputs[0]
    row_segs = segment_ids[0]
    row_cot = cotangent[0]
    cot_low = row_cot.astype(low)

    attn_flat = (w_query, w_key, w_value, w_out)
    attn_lengths = [w.shape[0] for w in attn_flat]
    got_attn, got_segs, all_cot = exchange(
        1, (pack(attn_flat), "ctx", "gather"), (segment_ids, "ctx", "gather"), (cot_low, "dp", "gather")
    )
    all_cot = all_cot.reshape(-1, D)
    all_segs = got_segs.reshape(seq_rows)
    slabs = unpack(got_attn, attn_lengths, (H * HD, KV * HD, KV * HD, D))
    mat_qkv, mat_out, got_gate_up = exchange(
        2,
        (jnp.concatenate(slabs[:3], axis=1), "dp", "gather"),
        (slabs[3], "dp", "gather"),
        (pack((w_gate, w_up)), "ctx", "gather"),
    )
    mat_qkv = mat_qkv.reshape(D, -1)
    mat_out = mat_out.reshape(H * HD, D)
    ff_part = FF // dp_count
    d_part = D // dp_count
    gate_slab, up_slab = (
        slab.reshape(d_part, dp_count, ff_part).transpose(1, 0, 2)
        for slab in unpack(got_gate_up, (w_gate.shape[0], w_up.shape[0]), (FF, FF))
    )

    inv_attn = lax.rsqrt(jnp.mean(row_input * row_input, axis=-1, keepdims=True) + norm_epsilon)
    normed_attn = (row_input * inv_attn * gain_attn).astype(low)
    qkv = matmul(normed_attn, mat_qkv)
    turned = rotate(
        qkv[:, : (H + KV) * HD].reshape(span_rows, H + KV, HD), cos_table, sin_table, 1.0
    ).astype(low)
    grouped_q = turned[:, :H].reshape(span_rows, KV, head_group, HD)
    packed_kv = jnp.concatenate(
        [turned[:, H:].reshape(span_rows, KV * HD), qkv[:, (H + KV) * HD :].astype(low)], axis=1
    )
    all_kv, mat_gate = exchange(3, (packed_kv, "ctx", "gather"), (gate_slab, "dp", "swap"))
    mat_gate = mat_gate.reshape(D, ff_part)
    all_kv = all_kv.reshape(seq_rows, 2 * KV * HD)
    all_keys = all_kv[:, : KV * HD].reshape(seq_rows, KV, HD)
    all_vals = all_kv[:, KV * HD :].reshape(seq_rows, KV, HD)

    def masked_scores(first_row, rows):
        block_keys = all_keys[first_row : first_row + rows]
        scores = (
            jnp.einsum("qkgd,skd->kgqs", grouped_q, block_keys, preferred_element_type=jnp.float32)
            * scale_factor
        )
        key_pos = first_row + jnp.arange(rows, dtype=jnp.int32)
        allowed = (row_segs[:, None] == all_segs[None, first_row : first_row + rows]) & (
            key_pos[None, :] <= query_pos[:, None]
        )
        return jnp.where(allowed[None, None], scores, -jnp.inf)

    scores = masked_scores(0, seq_rows)
    final_max = jnp.max(scores, axis=-1)
    weights_now = jnp.exp(scores - final_max[..., None])
    final_sum = jnp.sum(weights_now, axis=-1)
    final_acc = jnp.einsum(
        "kgqs,skd->kgqd", weights_now.astype(low), all_vals, preferred_element_type=jnp.float32
    )
    log_total = final_max + jnp.log(final_sum)
    attn = (
        (final_acc / final_sum[..., None])
        .transpose(2, 0, 1, 3)
        .reshape(span_rows, H * HD)
        .astype(low)
    )
    hidden = row_input + matmul(attn, mat_out)
    inv_ffn = lax.rsqrt(jnp.mean(hidden * hidden, axis=-1, keepdims=True) + norm_epsilon)
    normed_ffn = (hidden * inv_ffn * gain_ffn).astype(low)

    all_normed, got_down, mat_up = exchange(
        4,
        (normed_ffn, "dp", "gather"),
        (pack((w_down,)), "ctx", "gather"),
        (up_slab, "dp", "swap"),
    )
    mat_up = mat_up.reshape(D, ff_part)
    (mat_down,) = unpack(got_down, (w_down.shape[0],), (D,))
    all_normed = all_normed.reshape(-1, D)
    gate = matmul(all_normed, mat_gate)
    up_proj = matmul(all_normed, mat_up)
    sigma = jax.nn.sigmoid(gate)
    mixed = (gate * sigma * up_proj).astype(low)
    part_out = matmul(mixed, mat_down).astype(low).reshape(dp_count, span_rows, D)
    grad_mixed = matmul(all_cot, mat_down.T)
    grad_up = (grad_mixed * gate * sigma).astype(low)
    grad_gate = (grad_mixed * up_proj * sigma * (1.0 + gate * (1.0 - sigma))).astype(low)
    part_normed = matmul(grad_gate, mat_gate.T) + matmul(grad_up, mat_up.T)
    part_normed = part_normed.astype(low).reshape(dp_count, span_rows, D)
    grad_down = matmul(mixed.T, all_cot).astype(low)
    grad_mat_gate = matmul(all_normed.T, grad_gate).astype(low).reshape(dp_count, d_part, -1)
    grad_mat_up = matmul(all_normed.T, grad_up).astype(low).reshape(dp_count, d_part, -1)
    got_normed, got_down_grad, got_gate = exchange(
        5,
        (part_normed, "dp", "sum"),
        (pack_grads((grad_down,), ctx_count), "ctx", "sum"),
        (grad_mat_gate, "dp", "swap"),
    )
    grad_normed_ffn = total_of(got_normed)

    grad_res_ffn, grad_gffn = norm_back(grad_normed_ffn, hidden, inv_ffn, gain_ffn)
    grad_hidden = row_cot + grad_res_ffn
    grad_hidden_low = grad_hidden.astype(low)
    grad_out = matmul(attn.T, grad_hidden_low)
    grad_attn = matmul(grad_hidden_low, mat_out.T).astype(low)
    grad_grouped = grad_attn.reshape(span_rows, KV, head_group, HD)
    delta = jnp.sum(
        grad_grouped.astype(jnp.float32)
        * attn.reshape(span_rows, KV, head_group, HD).astype(jnp.float32),
        axis=-1,
    ).transpose(1, 2, 0)

    grad_q_rot = 0.0
    key_terms = []
    for first_row in range(0, seq_rows, key_block):
        block_keys = all_keys[first_row : first_row + key_block]
        block_vals = all_vals[first_row : first_row + key_block]
        probs = jnp.exp(masked_scores(first_row, key_block) - log_total[..., None])
        grad_probs = jnp.einsum(
            "qkgd,skd->kgqs", grad_grouped, block_vals, preferred_element_type=jnp.float32
        )
        grad_scores = (probs * (grad_probs - delta[..., None])).astype(low)
        grad_q_rot = (
            grad_q_rot
            + jnp.einsum(
                "kgqs,skd->qkgd", grad_scores, block_keys, preferred_element_type=jnp.float32
            )
            * scale_factor
        )
        grad_k_block = (
            jnp.einsum("kgqs,qkgd->skd", grad_scores, grouped_q, preferred_element_type=jnp.float32)
            * scale_factor
        )
        grad_v_block = jnp.einsum(
            "kgqs,qkgd->skd", probs.astype(low), grad_grouped, preferred_element_type=jnp.float32
        )
        key_terms.append(
            jnp.concatenate(
                [
                    grad_k_block.reshape(key_block, KV * HD),
                    grad_v_block.reshape(key_block, KV * HD),
                ],
                axis=1,
            ).astype(low)
        )
    key_terms = jnp.concatenate(key_terms, axis=0).reshape(ctx_count, span_rows, 2 * KV * HD)
    got_terms, got_up = exchange(6, (key_terms, "ctx", "sum"), (grad_mat_up, "dp", "swap"))
    slab_gate = got_gate.transpose(1, 0, 2).reshape(d_part, FF)
    slab_up = got_up.transpose(1, 0, 2).reshape(d_part, FF)
    own_grads = total_of(got_terms)
    grad_qk = rotate(
        jnp.concatenate(
            [
                grad_q_rot.reshape(span_rows, H, HD),
                own_grads[:, : KV * HD].reshape(span_rows, KV, HD),
            ],
            axis=1,
        ),
        cos_table,
        sin_table,
        -1.0,
    )
    grad_qkv = jnp.concatenate(
        [grad_qk.reshape(span_rows, (H + KV) * HD).astype(low), own_grads[:, KV * HD :].astype(low)],
        axis=1,
    )
    grad_mat_qkv = matmul(normed_attn.T, grad_qkv)
    grad_normed_attn = matmul(grad_qkv, mat_qkv.T)
    grad_res_attn, grad_gattn = norm_back(grad_normed_attn, row_input, inv_attn, gain_attn)
    grad_rows = grad_hidden + grad_res_attn

    gain_terms = jnp.stack([grad_gattn, grad_gffn])
    got_gains, got_qkv, got_out_grad, got_gu_grad = exchange(
        7,
        (gain_terms, "dp", "gather"),
        (grad_mat_qkv.astype(low).reshape(dp_count, d_part, -1), "dp", "sum"),
        (grad_out.astype(low).reshape(dp_count, H * HD // dp_count, D), "dp", "sum"),
        (pack_grads((slab_gate, slab_up), ctx_count), "ctx", "sum"),
    )
    slab_qkv = total_of(got_qkv).astype(low)
    slab_out = total_of(got_out_grad).astype(low)
    attn_slabs = (
        slab_qkv[:, : H * HD],
        slab_qkv[:, H * HD : (H + KV) * HD],
        slab_qkv[:, (H + KV) * HD :],
        slab_out,
    )
    got_gains, got_out, got_attn_grad = exchange(
        8,
        (total_of(got_gains), "ctx", "gather"),
        (part_out, "dp", "sum"),
        (pack_grads(attn_slabs, ctx_count), "ctx", "sum"),
    )
    gains = total_of(got_gains)
    out_rows = hidden + total_of(got_out)
    reduced = (
        unpack_grads(total_of(got_attn_grad), attn_lengths)
        + unpack_grads(total_of(got_gu_grad), (w_gate.shape[0], w_up.shape[0]))
        + unpack_grads(total_of(got_down_grad), (w_down.shape[0],))
    )
    return (out_rows[None], grad_rows[None], gains[0], gains[1], *reduced)


def solution(mesh):
    return jax.shard_map(
        on_device,
        mesh=mesh,
        in_specs=(
            P("dp", "ctx", None),
            P("dp", "ctx"),
            P(),
            P(),
            P(("dp", "ctx")),
            P(("dp", "ctx")),
            P(("dp", "ctx")),
            P(("dp", "ctx")),
            P(("dp", "ctx")),
            P(("dp", "ctx")),
            P(("dp", "ctx")),
            P("dp", "ctx", None),
        ),
        out_specs=(
            P("dp", "ctx", None),
            P("dp", "ctx", None),
            P(),
            P(),
            P(("dp", "ctx")),
            P(("dp", "ctx")),
            P(("dp", "ctx")),
            P(("dp", "ctx")),
            P(("dp", "ctx")),
            P(("dp", "ctx")),
            P(("dp", "ctx")),
        ),
        check_vma=False,
    )
```
